32 devices in a mesh: expert: 8 (over z, x), dp: 4 (over y, core).
Axes of the slice: x: 2, y: 2, z: 4, core: 2. Of those that a mesh axis runs over, the one named last changes fastest.
Arguments:
- features: bfloat16 [4096, 32, 64], P(('expert', 'dp')), may hold values from -1 to 1
- spacing: float32 [4096, 32], P(('expert', 'dp')), may hold values from 0.02 to 0.3
- targets: float32 [3, 4096], P(None, ('expert', 'dp')), may hold values from 0 to 1
- ray_length: int32 [4096], P(('expert', 'dp')), may hold values from 1 to 32, as said below
- cell_id: int32 [4096, 32], P(('expert', 'dp')), may hold values from 0 to 15, as said below
- slot_rank: int32 [4096, 32], P(('expert', 'dp')), may hold values from -1 to 383, as said below
- image_id: int32 [4096], P(('expert', 'dp')), may hold values from 0 to 511, as said below
- params: float32 [16, 848, 256], P('expert'), may hold values from -5 to 5
- first_moment: float32 [16, 848, 256], P('expert'), may hold values from -0.75 to 0.75
- second_moment: float32 [16, 848, 256], P('expert'), may hold values from 1e-06 to 0.01
- code_table: float32 [512, 64], P(('expert', 'dp')), may hold values from -6 to 6
- table_first: float32 [512, 64], P(('expert', 'dp')), may hold values from -0.75 to 0.75
- table_second: float32 [512, 64], P(('expert', 'dp')), may hold values from 1e-06 to 0.01
Outputs:
- ray_loss: float32 [4096], P(('expert', 'dp'))
- new_params: float32 [16, 848, 256], P('expert')
- new_first_moment: float32 [16, 848, 256], P('expert')
- new_second_moment: float32 [16, 848, 256], P('expert')
- new_code_table: float32 [512, 64], P(('expert', 'dp'))
- new_table_first: float32 [512, 64], P(('expert', 'dp'))
- new_table_second: float32 [512, 64], P(('expert', 'dp'))
The draws below stay inside these ranges and needn't reach their ends.
Inputs may be any that keep to these rules, and one draw needn't show every extreme that they name: `ray_length`: rays form aligned blocks of 128, one a device, in the order of the axes expert then dp. In every block the lengths sum to 3072 and some ray has all 32 samples. `cell_id`: also given for samples at or beyond their ray's length, where it is unused. `slot_rank`: for a sample below its ray's length: its rank among the live samples of its block of 128 rays that have the same cell_id, counted ray by ray and along each ray; -1 for the other samples. No block has more than 384 live samples of one cell_id; in every block some cell_id has exactly 384, and one cell_id has 384 in every block. `image_id`: A ray of block b names an image from b * 16 to (b + 1) * 16 - 1.
All inputs are finite; a program needn't handle non-finite values.
Results may differ from the reference program's by a relative error of at most 0.0046.
Values may be sent and summed in bfloat16 or wider, within the bound.
A program may use at most 128 MiB of HBM per device.

```python
import math
import jax
import jax.numpy as jnp
from jax import lax

NET_WIDTH = 256
CODE_WIDTH = 64
ENC_WIDTH = 64
LAYERS = 4
SAMPLES = 32
IMG_DEV = 16
RAY_DEV = 128
EXPERTS = 16
RAY_TOTAL = 4096
IMAGES = 512
LIVE_DEV = 3072
CAPACITY = 384
PARAM_ROWS = 848


def sample_layout(key):
    blocks = RAY_TOTAL // RAY_DEV
    hot_all = jax.random.randint(jax.random.fold_in(key, 11), (), 0, EXPERTS)

    def one_block(block_number):
        subkeys = jax.random.split(jax.random.fold_in(key, block_number), 7)
        drop_units = RAY_DEV * (SAMPLES - 1)
        unit_ray = jnp.arange(drop_units, dtype=jnp.int32) // (SAMPLES - 1)
        full_ray = jax.random.randint(subkeys[0], (), 0, RAY_DEV)
        shuffled = jax.random.permutation(subkeys[1], drop_units).astype(jnp.int32)
        ranking = shuffled + jnp.where(unit_ray == full_ray, drop_units, 0).astype(jnp.int32)
        picked = jnp.argsort(ranking)[:RAY_DEV * SAMPLES // 4]
        dropped = jnp.zeros((RAY_DEV,), jnp.int32).at[unit_ray[picked]].add(1)
        lengths = (SAMPLES - dropped).astype(jnp.int32)
        pair_count = EXPERTS * CAPACITY
        pair_cell = jnp.arange(pair_count, dtype=jnp.int32) // CAPACITY
        own_hot = jax.random.randint(subkeys[2], (), 0, EXPERTS)
        cell_bias = jax.random.randint(subkeys[3], (EXPERTS,), 0, 4)
        cell_range = jnp.arange(EXPERTS, dtype=jnp.int32)
        cell_bias = jnp.where((cell_range == hot_all) | (cell_range == own_hot), 16, cell_bias).astype(jnp.int32)
        pair_score = cell_bias[pair_cell] * (pair_count // 4) + jax.random.permutation(subkeys[4], pair_count).astype(jnp.int32)
        chosen = pair_cell[jnp.argsort(-pair_score)[:LIVE_DEV]]
        chosen = chosen[jax.random.permutation(subkeys[5], LIVE_DEV)]
        position = jnp.arange(SAMPLES, dtype=jnp.int32)
        flat_live = (position[None, :] < lengths[:, None]).reshape(RAY_DEV * SAMPLES)
        rank_live = jnp.cumsum(flat_live.astype(jnp.int32)) - 1
        dead_cell = jax.random.randint(subkeys[6], (RAY_DEV * SAMPLES,), 0, EXPERTS)
        cell_ids = jnp.where(flat_live, chosen[jnp.clip(rank_live, 0, LIVE_DEV - 1)], dead_cell).astype(jnp.int32)
        onehot = (cell_ids[:, None] == cell_range[None, :]) & flat_live[:, None]
        counts = jnp.cumsum(onehot.astype(jnp.int32), axis=0) - 1
        slot_ranks = jnp.where(flat_live, jnp.take_along_axis(counts, cell_ids[:, None], axis=1)[:, 0], -1).astype(jnp.int32)
        return (lengths, cell_ids.reshape(RAY_DEV, SAMPLES), slot_ranks.reshape(RAY_DEV, SAMPLES))
    lengths, cell_ids, slot_ranks = lax.map(one_block, jnp.arange(blocks, dtype=jnp.int32))
    return (lengths.reshape(RAY_TOTAL), cell_ids.reshape(RAY_TOTAL, SAMPLES), slot_ranks.reshape(RAY_TOTAL, SAMPLES))


def draw_ray_length(key, part):
    return sample_layout(jax.random.fold_in(key, 5))[0]


def draw_cell_id(key, part):
    return sample_layout(jax.random.fold_in(key, 5))[1]


def draw_slot_rank(key, part):
    return sample_layout(jax.random.fold_in(key, 5))[2]


def draw_image_id(key, part):
    blocks = RAY_TOTAL // RAY_DEV
    local_ids = jax.random.randint(key, (blocks, RAY_DEV), 0, IMG_DEV)
    marked = jax.random.randint(jax.random.fold_in(key, 3), (blocks, 2), 0, RAY_DEV)
    row_number = jnp.arange(blocks, dtype=jnp.int32)
    local_ids = local_ids.at[row_number, marked[:, 1]].set(0)
    local_ids = local_ids.at[row_number, marked[:, 0]].set(IMG_DEV - 1)
    global_ids = local_ids + (row_number * IMG_DEV)[:, None]
    return global_ids.reshape(RAY_TOTAL).astype(jnp.int32)


def draw_params(key, part):
    head_row = ENC_WIDTH + (LAYERS - 1) * NET_WIDTH
    row_number = jnp.arange(PARAM_ROWS)
    row_scale = jnp.where(row_number < ENC_WIDTH, (2.0 / ENC_WIDTH) ** 0.5, (2.0 / NET_WIDTH) ** 0.5)
    row_scale = jnp.where(row_number >= head_row, NET_WIDTH ** (-0.5), row_scale)
    row_scale = jnp.where(row_number >= head_row + 4, 4.0 * CODE_WIDTH ** (-0.5), row_scale)
    row_scale = jnp.where(row_number >= head_row + 8, 0.3, row_scale)
    normals = jnp.clip(jax.random.normal(key, (EXPERTS, PARAM_ROWS, NET_WIDTH), jnp.float32), -5.0, 5.0)
    return normals * row_scale[None, :, None].astype(jnp.float32)


def levels(rng, shape, cuts, least, top_value):
    gain = 1.0
    for dim, parts in cuts:
        heights = jax.random.uniform(jax.random.fold_in(jax.random.fold_in(rng, 6), dim), (parts,), jnp.float32, least / len(cuts), top_value / len(cuts))
        gain = gain * jnp.repeat(jnp.exp(heights), shape[dim] // parts).reshape((-1,) + (1,) * (len(shape) - 1 - dim))
    return gain


def normal_values(stream_key, dims, deviation, limit, shards=(), kind=jnp.bfloat16):
    level = levels(stream_key, dims, shards, -0.22, 0.18) if shards else 1.0
    values = jax.random.normal(stream_key, dims, jnp.float32) * deviation * level
    return jnp.minimum(jnp.maximum(values, -limit), limit).astype(kind)


def setup_inputs(seed: int = 0) -> dict:
    key_list = jax.random.split(jax.random.key(seed), 14)
    return {
        "features": jnp.clip(jax.random.uniform(key_list[0], (RAY_TOTAL, SAMPLES, ENC_WIDTH), jnp.float32, -1.0, 1.0) * levels(key_list[0], (RAY_TOTAL, SAMPLES, ENC_WIDTH), ((0, 32),), -0.4, 0.0), -1.0, 1.0).astype(jnp.bfloat16),
        "spacing": jnp.clip(jnp.exp(math.log(0.3) - 2.7080503 * jax.random.uniform(key_list[1], (RAY_TOTAL, SAMPLES), jnp.float32) ** levels(key_list[1], (RAY_TOTAL, SAMPLES), ((0, 32),), -0.2, 0.2)), 0.02, 0.3),
        "targets": jnp.clip(1.0 * jax.random.uniform(key_list[2], (3, RAY_TOTAL), jnp.float32) ** levels(key_list[2], (3, RAY_TOTAL), ((1, 32),), -0.2, 0.2), 0.0, 1.0),
        "ray_length": draw_ray_length(jax.random.fold_in(key_list[13], 71), 0),
        "cell_id": draw_cell_id(jax.random.fold_in(key_list[13], 71), 0),
        "slot_rank": draw_slot_rank(jax.random.fold_in(key_list[13], 71), 0),
        "image_id": draw_image_id(jax.random.fold_in(key_list[13], 71), 0),
        "params": draw_params(jax.random.fold_in(key_list[13], 71), 0),
        "first_moment": normal_values(key_list[8], (EXPERTS, PARAM_ROWS, NET_WIDTH), 0.05, 0.75, ((0, 8),), jnp.float32),
        "second_moment": jnp.clip(jnp.exp(math.log(0.01) - 9.2103404 * jax.random.uniform(key_list[9], (EXPERTS, PARAM_ROWS, NET_WIDTH), jnp.float32) ** levels(key_list[9], (EXPERTS, PARAM_ROWS, NET_WIDTH), ((0, 8),), -0.2, 0.2)), 9.999999974752427e-07, 0.01),
        "code_table": normal_values(key_list[10], (IMAGES, CODE_WIDTH), 0.5, 6.0, ((0, 32),), jnp.float32),
        "table_first": normal_values(key_list[11], (IMAGES, CODE_WIDTH), 0.05, 0.75, ((0, 32),), jnp.float32),
        "table_second": jnp.clip(jnp.exp(math.log(0.01) - 9.2103404 * jax.random.uniform(key_list[12], (IMAGES, CODE_WIDTH), jnp.float32) ** levels(key_list[12], (IMAGES, CODE_WIDTH), ((0, 32),), -0.2, 0.2)), 9.999999974752427e-07, 0.01),
    }


BETA_ONE = 0.9
BETA_TWO = 0.999
LEARN_RATE = 0.001
ADAM_EPS = 1e-08
CORRECT_ONE = 1.0 - 0.9 ** 10
CORRECT_TWO = 1.0 - 0.999 ** 10

def adam_update(param_now, gradient, moment_one, moment_two):
    new_one = BETA_ONE * moment_one + (1.0 - BETA_ONE) * gradient
    new_two = BETA_TWO * moment_two + (1.0 - BETA_TWO) * gradient * gradient
    update = LEARN_RATE * (new_one / CORRECT_ONE) / (jnp.sqrt(new_two / CORRECT_TWO) + ADAM_EPS)
    return (param_now - update, new_one, new_two)

def composite(raw_out, spacing, live_mask, targets):
    density = jax.nn.softplus(raw_out[0])
    colors = jax.nn.sigmoid(raw_out[1:4])
    optical = density * spacing * live_mask
    before = jnp.cumsum(optical, axis=1) - optical
    weight = jnp.exp(-before) * (1.0 - jnp.exp(-optical))
    render = lax.optimization_barrier(jnp.sum(weight[None] * colors, axis=2))
    return 0.5 * lax.optimization_barrier(jnp.sum((render - targets) ** 2, axis=0))

def contract_first(left, right):
    return lax.dot_general(left.astype(jnp.float32), right.astype(jnp.float32), (((0,), (0,)), ((), ())))

def contract_last(left, right):
    return lax.dot_general(left.astype(jnp.float32), right.astype(jnp.float32), (((1,), (1,)), ((), ())))

def expert_forward(weights, inputs, code_rows):
    head_row = ENC_WIDTH + (LAYERS - 1) * NET_WIDTH
    activations = [inputs]
    preacts = []
    current = inputs
    row_start = 0
    row_count = ENC_WIDTH
    for layer_index in range(LAYERS):
        matrix = weights[row_start:row_start + row_count]
        preact = jnp.dot(current.astype(jnp.float32), matrix.astype(jnp.float32)) + weights[head_row + 9 + layer_index].astype(jnp.float32)
        current = jnp.maximum(preact, 0.0).astype(jnp.bfloat16)
        preacts.append(preact)
        activations.append(current)
        row_start = row_start + row_count
        row_count = NET_WIDTH
    hidden_part = contract_last(current, weights[head_row:head_row + 4])
    code_part = contract_last(code_rows, weights[head_row + 4:head_row + 8, :CODE_WIDTH])
    raw_out = hidden_part + code_part + weights[head_row + 8, :4].astype(jnp.float32)
    return (activations, preacts, raw_out)

def expert_backward(weights, activations, preacts, code_rows, cotangent):
    head_row = ENC_WIDTH + (LAYERS - 1) * NET_WIDTH
    hidden_head = contract_first(cotangent, activations[-1])
    code_head = contract_first(cotangent, code_rows)
    bias_head = lax.optimization_barrier(jnp.sum(cotangent.astype(jnp.float32), axis=0))
    code_grad = jnp.dot(cotangent.astype(jnp.float32), weights[head_row + 4:head_row + 8, :CODE_WIDTH].astype(jnp.float32))
    upstream = jnp.dot(cotangent.astype(jnp.float32), weights[head_row:head_row + 4].astype(jnp.float32))
    weight_grads = [None] * LAYERS
    bias_grads = [None] * LAYERS
    for layer_index in reversed(range(LAYERS)):
        pre_grad = jnp.where(preacts[layer_index] > 0, upstream, 0.0).astype(jnp.bfloat16)
        weight_grads[layer_index] = contract_first(activations[layer_index], pre_grad)
        bias_grads[layer_index] = lax.optimization_barrier(jnp.sum(pre_grad.astype(jnp.float32), axis=0))
        if layer_index > 0:
            row_start = ENC_WIDTH + (layer_index - 1) * NET_WIDTH
            upstream = contract_last(pre_grad, weights[row_start:row_start + NET_WIDTH])
    pieces = list(weight_grads) + [hidden_head, jnp.pad(code_head, ((0, 0), (0, NET_WIDTH - CODE_WIDTH))), jnp.pad(bias_head, (0, NET_WIDTH - 4))[None, :], jnp.stack(bias_grads, axis=0), jnp.zeros((7 - LAYERS, NET_WIDTH), jnp.float32)]
    return (jnp.concatenate(pieces, axis=0), code_grad)

def reference(features, spacing, targets, ray_length, cell_id, slot_rank, image_id, params, first_moment, second_moment, code_table, table_first, table_second):
    ray_total = features.shape[0]
    sample_count = ray_total * SAMPLES
    blocks = ray_total // RAY_DEV
    column_count = blocks * CAPACITY
    positions = features.reshape(sample_count, ENC_WIDTH)
    ray_code = code_table.astype(jnp.bfloat16)[image_id]
    sample_code = jnp.broadcast_to(ray_code[:, None, :], (ray_total, SAMPLES, CODE_WIDTH)).reshape(sample_count, CODE_WIDTH)
    flat_rank = slot_rank.reshape(sample_count)
    flat_cell = cell_id.reshape(sample_count)
    sample_numbers = jnp.arange(sample_count, dtype=jnp.int32)
    block_number = sample_numbers // (RAY_DEV * SAMPLES)
    column = jnp.where(flat_rank >= 0, block_number * CAPACITY + flat_rank, column_count).astype(jnp.int32)
    owner_ids = jnp.full((EXPERTS, column_count), -1, jnp.int32).at[flat_cell, column].set(sample_numbers, mode='drop')
    weights_bf = params.astype(jnp.bfloat16)

    def gather_rows(sample_ids):
        occupied = sample_ids >= 0
        safe_ids = jnp.maximum(sample_ids, 0)
        inputs = jnp.where(occupied[:, None], positions[safe_ids], jnp.zeros((), jnp.bfloat16))
        code_rows = jnp.where(occupied[:, None], sample_code[safe_ids], jnp.zeros((), jnp.bfloat16))
        return (occupied, safe_ids, inputs, code_rows)

    def forward_one(operands):
        weights, sample_ids = operands
        occupied, safe_ids, inputs, code_rows = gather_rows(sample_ids)
        return expert_forward(weights, inputs, code_rows)[2]
    raw_table = lax.map(forward_one, (weights_bf, owner_ids))
    live_flat = flat_rank >= 0
    raw_samples = raw_table[flat_cell, jnp.minimum(column, column_count - 1)]
    raw_samples = jnp.where(live_flat[:, None], raw_samples, 0.0)
    position = jnp.arange(SAMPLES, dtype=jnp.int32)
    live_mask = (position[None, :] < ray_length[:, None]).astype(jnp.float32)
    raw_grid = raw_samples.T.reshape(4, ray_total, SAMPLES)

    def loss_of(raw_in):
        return composite(raw_in, spacing, live_mask, targets)
    ray_loss, pullback = jax.vjp(loss_of, raw_grid)
    raw_grad, = pullback(jnp.ones_like(ray_loss))
    cotangent = raw_grad.reshape(4, sample_count).T.astype(jnp.bfloat16)

    def backward_one(code_sum, operands):
        weights, sample_ids = operands
        occupied, safe_ids, inputs, code_rows = gather_rows(sample_ids)
        upstream_rows = jnp.where(occupied[:, None], cotangent[safe_ids], jnp.zeros((), jnp.bfloat16))
        activations, preacts, raw_out = expert_forward(weights, inputs, code_rows)
        gradient, code_grad = expert_backward(weights, activations, preacts, code_rows, upstream_rows)
        code_sum = code_sum.at[safe_ids // SAMPLES].add(jnp.where(occupied[:, None], code_grad, 0.0))
        return (code_sum, gradient)
    ray_code_grad, param_grad = lax.scan(backward_one, jnp.zeros((ray_total, CODE_WIDTH), jnp.float32), (weights_bf, owner_ids))
    table_grad = jax.ops.segment_sum(ray_code_grad, image_id, num_segments=IMAGES)
    new_params, new_first, new_second = adam_update(params, param_grad, first_moment, second_moment)
    new_table, new_table_first, new_table_second = adam_update(code_table, table_grad, table_first, table_second)
    return (ray_loss, new_params, new_first, new_second, new_table, new_table_first, new_table_second)
```

```python
import functools

import jax
import jax.numpy as jnp
from jax import lax
from jax.experimental import pallas as pl
from jax.experimental.pallas import tpu as pltpu
from jax.sharding import PartitionSpec as P

NET_WIDTH = 256
CODE_WIDTH = 64
ENC_WIDTH = 64
LAYERS = 4
SAMPLES = 32
HEAD_ROW = ENC_WIDTH + (LAYERS - 1) * NET_WIDTH
LANES = 128

BETA_ONE = 0.9
BETA_TWO = 0.999
LEARN_RATE = 0.001
ADAM_EPS = 1e-08
CORRECT_ONE = 1.0 - 0.9**10
CORRECT_TWO = 1.0 - 0.999**10

MESH = pl.DeviceIdType.MESH
VMEM = pl.BlockSpec(memory_space=pltpu.VMEM)
SMEM = pl.BlockSpec(memory_space=pltpu.SMEM)
F32 = jnp.float32
BF16 = jnp.bfloat16
NN = (((1,), (0,)), ((), ()))
NT = (((1,), (1,)), ((), ()))
TN = (((0,), (0,)), ((), ()))


def dot(left, right, dims=NN, precision=None):
    return lax.dot_general(left, right, dims, precision=precision, preferred_element_type=F32)


def exact(left, right, dims=NN):
    return dot(left, right, dims, lax.Precision.HIGHEST)


def adam_update(param_now, gradient, moment_one, moment_two):
    new_one = BETA_ONE * moment_one + (1.0 - BETA_ONE) * gradient
    new_two = BETA_TWO * moment_two + (1.0 - BETA_TWO) * gradient * gradient
    update = LEARN_RATE * (new_one / CORRECT_ONE) / (jnp.sqrt(new_two / CORRECT_TWO) + ADAM_EPS)
    return (param_now - update, new_one, new_two)


def lane_block(index):
    return pl.ds(pl.multiple_of(index * LANES, LANES), LANES)


def move_rows(count, move):
    step = 32

    def body(block, carry):
        for inner in range(step):
            move(block * step + inner)
        return carry

    lax.fori_loop(0, count // step, body, 0)


def place_kernel(groups, cap, cap_up, slot_ref, feat_ref, out_ref, rows, table):
    table[...] = jnp.zeros_like(table)

    def turn(i, carry):
        block = feat_ref[i].astype(F32)
        rows[lane_block(i), :] = jnp.concatenate([block, block], axis=0).T
        return carry

    lax.fori_loop(0, SAMPLES, turn, 0)

    def move(s):
        table[pl.ds(slot_ref[s], 1), :] = rows[pl.ds(s, 1), :]

    move_rows(rows.shape[0], move)
    low = lax.broadcasted_iota(jnp.int32, (cap, LANES), 1) < ENC_WIDTH

    def pack(g, carry):
        first = table[pl.ds(pl.multiple_of(2 * g * cap_up, LANES), cap), :]
        second = table[pl.ds(pl.multiple_of((2 * g + 1) * cap_up, LANES), cap), :]
        out_ref[g] = jnp.where(low, first, second).astype(BF16)
        return carry

    lax.fori_loop(0, groups, pack, 0)


def greet(groups, me):
    barrier = pltpu.get_barrier_semaphore()

    def body(k, carry):
        pl.semaphore_signal(
            barrier, 1, device_id={"expert": lax.rem(me + k, groups)}, device_id_type=MESH
        )
        return carry

    lax.fori_loop(1, groups, body, 0)
    return barrier


def pad_first(wt_ref, m0):
    m0[...] = jnp.zeros_like(m0)
    for h in range(2):
        m0[h, ENC_WIDTH * h : ENC_WIDTH * (h + 1), :] = wt_ref[h, 0:ENC_WIDTH, :]


def layer_matrix(wt_ref, m0, h, layer):
    if layer == 0:
        return m0[h]
    start = ENC_WIDTH + (layer - 1) * NET_WIDTH
    return wt_ref[h, start : start + NET_WIDTH, :]


def tail_rows(wt_ref, h):
    return wt_ref[h, HEAD_ROW : HEAD_ROW + 16, :]


def forward(wt_ref, m0, h, current, keep=None):
    tail = tail_rows(wt_ref, h).astype(F32)
    for layer in range(LAYERS):
        preact = dot(current, layer_matrix(wt_ref, m0, h, layer))
        preact = preact + tail[9 + layer : 10 + layer, :]
        current = jnp.maximum(preact, 0.0).astype(BF16)
        if keep is not None:
            keep(layer, current)
    return current


def forward_kernel(
    groups, cap, cap_up, disp, wt, tail_msg, arr, raw_out, recv, msg, back, m0, s1, r1, s2, r2
):
    me = lax.axis_index("expert")
    barrier = greet(groups, me)
    pl.semaphore_wait(barrier, groups - 1)

    def out_copy(k):
        peer = lax.rem(me + k, groups)
        return pltpu.make_async_remote_copy(
            disp.at[peer], recv.at[k], s1.at[k], r1.at[k],
            device_id={"expert": peer}, device_id_type=MESH,
        )

    def back_copy(k):
        peer = lax.rem(me + groups - k, groups)
        return pltpu.make_async_remote_copy(
            msg.at[k], back.at[me], s2.at[k], r2.at[k],
            device_id={"expert": peer}, device_id_type=MESH,
        )

    def start(k, carry):
        out_copy(k).start()
        return carry

    lax.fori_loop(1, groups, start, 0)
    pad_first(wt, m0)

    def process(k, block):
        arr[k] = block
        msg[k, :, cap_up:] = tail_msg[...]
        if cap_up > cap:
            msg[k, :, cap:cap_up] = jnp.zeros((8, cap_up - cap), F32)
        for h in range(2):
            act = forward(wt, m0, h, block)
            raw = dot(tail_rows(wt, h), act, NT)
            msg[k, 4 * h : 4 * h + 4, 0:cap] = raw[0:4]

    process(0, disp[me])
    back[me] = msg[0]

    def step(k, carry):
        out_copy(k).wait_recv()
        process(k, recv[k])
        back_copy(k).start()
        return carry

    lax.fori_loop(1, groups, step, 0)

    def finish(k, carry):
        out_copy(k).wait_send()
        back_copy(k).wait_send()
        back_copy(k).wait_recv()
        return carry

    lax.fori_loop(1, groups, finish, 0)
    raw_out[...] = back[...]


def home_kernel(
    groups, cap_up, slot_ref, raw_ref, cell_ref, spacing_ref, length_ref, target_ref, image_ref,
    code_ref, first_ref, second_ref, loss_out, msg_out, code_out, first_out, second_out,
    rows, table, eight, mix, queries, shift,
):
    tiles = cap_up // LANES
    filler = jnp.zeros((LANES - 8, LANES), F32)

    def widen(g, carry):
        for t in range(tiles):
            piece = raw_ref[g, :, t * LANES : (t + 1) * LANES]
            turned = jnp.concatenate([piece, filler], axis=0).T
            for h in range(2):
                start = pl.multiple_of((2 * g + h) * cap_up + t * LANES, LANES)
                table[pl.ds(start, LANES), :] = turned
        block = pl.ds(pl.multiple_of(8 * g, 8), 8)
        queries[block, :] = raw_ref[g, :, cap_up : cap_up + CODE_WIDTH]
        shift[block, :] = jnp.broadcast_to(
            raw_ref[g, :, cap_up + CODE_WIDTH : cap_up + CODE_WIDTH + 1], (8, LANES)
        )
        return carry

    lax.fori_loop(0, groups, widen, 0)
    table[pl.ds(2 * groups * cap_up, 8), :] = jnp.zeros((8, LANES), F32)

    def take(s):
        rows[pl.ds(s, 1), :] = table[pl.ds(slot_ref[s], 1), :]

    move_rows(rows.shape[0], take)

    def narrow(i, carry):
        eight[pl.ds(pl.multiple_of(8 * i, 8), 8), :] = rows[lane_block(i), :].T[0:8]
        return carry

    lax.fori_loop(0, SAMPLES, narrow, 0)
    table[...] = jnp.zeros_like(table)

    table_rows = code_ref.shape[0]
    pick = (
        lax.broadcasted_iota(jnp.int32, (table_rows, LANES), 0) == image_ref[...]
    ).astype(F32)
    code_bf = code_ref[...].astype(BF16).astype(F32)
    ray_code = exact(code_bf, pick, TN)
    mix[...] = exact(queries[...], ray_code) + shift[...]

    cell = cell_ref[...]
    odd = lax.rem(cell, 2) == 1
    row = lax.broadcasted_iota(jnp.int32, (SAMPLES, LANES), 0)
    live = row < length_ref[...]
    raws = tuple(
        jnp.where(
            odd, eight[pl.ds(4 + c, SAMPLES, 8), :], eight[pl.ds(c, SAMPLES, 8), :]
        )
        for c in range(4)
    )

    def add_code(g, raws):
        part = mix[pl.ds(pl.multiple_of(8 * g, 8), 8), :]
        raws = list(raws)
        for h in range(2):
            hit = cell == 2 * g + h
            for c in range(4):
                j = 4 * h + c
                raws[c] = raws[c] + jnp.where(hit, part[j : j + 1, :], 0.0)
        return tuple(raws)

    raws = lax.fori_loop(0, groups, add_code, raws)
    raws = [jnp.where(live, raw, 0.0) for raw in raws]
    spacing = spacing_ref[...]
    density = jnp.maximum(raws[0], 0.0) + jnp.log1p(jnp.exp(-jnp.abs(raws[0])))
    colors = [jax.nn.sigmoid(raw) for raw in raws[1:]]
    tau = jnp.where(live, density * spacing, 0.0)
    square_row = lax.broadcasted_iota(jnp.int32, (SAMPLES, SAMPLES), 0)
    square_col = lax.broadcasted_iota(jnp.int32, (SAMPLES, SAMPLES), 1)
    before = exact((square_col < square_row).astype(F32), tau)
    through = jnp.exp(-before)
    fade = jnp.exp(-tau)
    weight = through * (1.0 - fade)
    gaps = [
        jnp.sum(weight * colors[c], axis=0, keepdims=True) - target_ref[c : c + 1, :]
        for c in range(3)
    ]
    loss_out[...] = 0.5 * (gaps[0] * gaps[0] + gaps[1] * gaps[1] + gaps[2] * gaps[2])
    pull = gaps[0] * colors[0] + gaps[1] * colors[1] + gaps[2] * colors[2]
    after = exact((square_col > square_row).astype(F32), pull * weight)
    tau_grad = pull * through * fade - after
    grads = [tau_grad * spacing * jax.nn.sigmoid(raws[0])]
    for c in range(3):
        grads.append(gaps[c] * weight * colors[c] * (1.0 - colors[c]))
    cots = [jnp.where(live, grad, 0.0).astype(BF16).astype(F32) for grad in grads]
    for c in range(4):
        eight[pl.ds(c, SAMPLES, 8), :] = jnp.where(odd, 0.0, cots[c])
        eight[pl.ds(4 + c, SAMPLES, 8), :] = jnp.where(odd, cots[c], 0.0)

    def gather_code(g, carry):
        pieces = []
        for h in range(2):
            hit = cell == 2 * g + h
            for c in range(4):
                pieces.append(jnp.sum(jnp.where(hit, cots[c], 0.0), axis=0, keepdims=True))
        mix[pl.ds(pl.multiple_of(8 * g, 8), 8), :] = jnp.concatenate(pieces, axis=0)
        return carry

    lax.fori_loop(0, groups, gather_code, 0)
    totals = mix[...]
    query_grad = exact(totals, ray_code, NT)
    table_grad = exact(exact(totals, pick, NT), queries[...], TN)
    new_code, new_first, new_second = adam_update(
        code_ref[...], table_grad, first_ref[...], second_ref[...]
    )
    code_out[...] = new_code
    first_out[...] = new_first
    second_out[...] = new_second
    queries[...] = query_grad

    def widen_back(i, carry):
        piece = eight[pl.ds(pl.multiple_of(8 * i, 8), 8), :]
        rows[lane_block(i), :] = jnp.concatenate([piece, filler], axis=0).T
        return carry

    lax.fori_loop(0, SAMPLES, widen_back, 0)

    def put(s):
        table[pl.ds(slot_ref[s], 1), :] = rows[pl.ds(s, 1), :]

    move_rows(rows.shape[0], put)

    def pack(g, carry):
        for t in range(tiles):
            start = [pl.multiple_of((2 * g + h) * cap_up + t * LANES, LANES) for h in range(2)]
            both = table[pl.ds(start[0], LANES), :] + table[pl.ds(start[1], LANES), :]
            msg_out[g, :, t * LANES : (t + 1) * LANES] = both.T[0:8]
        part = queries[pl.ds(pl.multiple_of(8 * g, 8), 8), :]
        msg_out[g, :, cap_up:] = jnp.concatenate(
            [part, jnp.zeros((8, LANES - CODE_WIDTH), F32)], axis=1
        )
        return carry

    lax.fori_loop(0, groups, pack, 0)


def backward_kernel(
    groups, cap, cap_up, msg, wt, arr, grad_out, recv, act, pre, m0, head, code_sum, cot_sum,
    grad, half_in, sum_out, sum_in, full, s1, r1, s2, r2,
):
    me = lax.axis_index("expert")
    my_dp = lax.axis_index("dp")
    core = lax.rem(my_dp, 2)
    near = my_dp + 1 - 2 * core
    far = my_dp + 2 - 4 * lax.rem(my_dp // 2, 2)
    barrier = greet(groups, me)
    for peer in (near, far):
        pl.semaphore_signal(barrier, 1, device_id={"dp": peer}, device_id_type=MESH)
    pl.semaphore_wait(barrier, groups + 1)

    def out_copy(k):
        peer = lax.rem(me + k, groups)
        return pltpu.make_async_remote_copy(
            msg.at[peer], recv.at[k], s1.at[k], r1.at[k],
            device_id={"expert": peer}, device_id_type=MESH,
        )

    def start(k, carry):
        out_copy(k).start()
        return carry

    lax.fori_loop(1, groups, start, 0)
    pad_first(wt, m0)
    head[...] = jnp.zeros_like(head)
    for h in range(2):
        head[h, 4 * h : 4 * h + 4, :] = tail_rows(wt, h).astype(F32)[0:4]

    def again(k, carry):
        block = pl.ds(pl.multiple_of(k * cap, 16), cap)
        for h in range(2):

            def keep(layer, value):
                act[layer, h, block, :] = value

            forward(wt, m0, h, arr[block, :], keep)
        return carry

    lax.fori_loop(0, groups, again, 0)
    recv[0] = msg[me]

    def arrive(k, carry):
        out_copy(k).wait()
        return carry

    lax.fori_loop(1, groups, arrive, 0)

    chunks = []
    for layer in range(LAYERS):
        first = 0 if layer == 0 else ENC_WIDTH + (layer - 1) * NET_WIDTH
        last = HEAD_ROW + 16 if layer == LAYERS - 1 else ENC_WIDTH + layer * NET_WIDTH
        chunks.append(pl.ds(first, last - first))

    def near_copy(layer):
        return pltpu.make_async_remote_copy(
            grad.at[1 - core, chunks[layer]], half_in.at[chunks[layer]],
            s2.at[0, layer], r2.at[0, layer], device_id={"dp": near}, device_id_type=MESH,
        )

    def far_copy(layer):
        return pltpu.make_async_remote_copy(
            sum_out.at[chunks[layer]], sum_in.at[chunks[layer]],
            s2.at[1, layer], r2.at[1, layer], device_id={"dp": far}, device_id_type=MESH,
        )

    def full_copy(layer):
        return pltpu.make_async_remote_copy(
            full.at[core, chunks[layer]], full.at[core, chunks[layer]],
            s2.at[2, layer], r2.at[2, layer], device_id={"dp": near}, device_id_type=MESH,
        )

    def second_stage(layer):
        near_copy(layer).wait_recv()
        rows = chunks[layer]
        sum_out[rows, :] = (grad[core, rows, :] + half_in[rows, :]).astype(BF16)
        far_copy(layer).start()

    def third_stage(layer):
        far_copy(layer).wait_recv()
        rows = chunks[layer]
        full[core, rows, :] = sum_out[rows, :].astype(F32) + sum_in[rows, :].astype(F32)
        full_copy(layer).start()

    bias = [[None] * LAYERS for _ in range(2)]
    top = LAYERS - 1
    hidden = []

    for h in range(2):

        def back(k, carry):
            block = pl.ds(pl.multiple_of(k * cap, 16), cap)
            cot = recv[k, :, 0:cap].astype(BF16)
            up = dot(cot, head[h].astype(BF16), TN)
            sums = []
            for layer in reversed(range(LAYERS)):
                value = jnp.where(act[layer, h, block, :].astype(F32) > 0, up, 0.0).astype(BF16)
                pre[layer, h, block, :] = value
                sums.append(
                    carry[top - layer] + jnp.sum(value.astype(F32), axis=0, keepdims=True)
                )
                if layer > 0:
                    up = dot(value, layer_matrix(wt, m0, h, layer), NT)
            heads = carry[LAYERS] + dot(cot, act[top, h, block, :])
            return tuple(sums) + (heads,)

        zero = jnp.zeros((1, NET_WIDTH), F32)
        done = lax.fori_loop(
            0, groups, back, (zero,) * LAYERS + (jnp.zeros((8, NET_WIDTH), F32),)
        )
        for layer in range(LAYERS):
            bias[h][layer] = done[top - layer]
        hidden.append(done[LAYERS])

    code_sum[...] = jnp.zeros_like(code_sum)
    cot_sum[...] = jnp.zeros_like(cot_sum)

    def add_codes(k, carry):
        code_sum[...] += recv[k, :, cap_up:]
        cot_sum[...] += jnp.broadcast_to(
            jnp.sum(recv[k, :, 0:cap], axis=1, keepdims=True), (8, LANES)
        )
        return carry

    lax.fori_loop(0, groups, add_codes, 0)
    codes = jnp.concatenate([code_sum[...], jnp.zeros((8, NET_WIDTH - LANES), F32)], axis=1)
    spot = (
        lax.broadcasted_iota(jnp.int32, (8, LANES), 0)
        == lax.broadcasted_iota(jnp.int32, (8, LANES), 1)
    )
    cot_row = jnp.sum(jnp.where(spot, cot_sum[...], 0.0), axis=0, keepdims=True)
    lane = lax.broadcasted_iota(jnp.int32, (1, LANES), 1)
    for h in range(2):
        line = cot_row if h == 0 else pltpu.roll(cot_row, LANES - 4, 1)
        line = jnp.where(lane < 4, line, 0.0)
        line = jnp.concatenate([line, jnp.zeros((1, NET_WIDTH - LANES), F32)], axis=1)
        grad[h, HEAD_ROW : HEAD_ROW + 16, :] = jnp.concatenate(
            [hidden[h][4 * h : 4 * h + 4], codes[4 * h : 4 * h + 4], line]
            + bias[h]
            + [jnp.zeros((7 - LAYERS, NET_WIDTH), F32)],
            axis=0,
        )

    for layer in reversed(range(LAYERS)):
        first = 0 if layer == 0 else ENC_WIDTH + (layer - 1) * NET_WIDTH
        for h in range(2):
            if layer == 0:
                value = dot(arr[...], pre[0, h], TN)
                grad[h, 0:ENC_WIDTH, :] = value[ENC_WIDTH * h : ENC_WIDTH * (h + 1)]
            else:
                grad[h, first : first + NET_WIDTH, :] = dot(act[layer - 1, h], pre[layer, h], TN)
        near_copy(layer).start()
        if layer < top:
            second_stage(layer + 1)
        if layer < top - 1:
            third_stage(layer + 2)
    second_stage(0)
    third_stage(1)
    third_stage(0)
    for layer in reversed(range(LAYERS)):
        near_copy(layer).wait_send()
        far_copy(layer).wait_send()
        full_copy(layer).wait_send()
        other = pltpu.make_async_remote_copy(
            full.at[1 - core, chunks[layer]], full.at[1 - core, chunks[layer]],
            s2.at[2, layer], r2.at[2, layer], device_id={"dp": near}, device_id_type=MESH,
        )
        other.wait_recv()
        grad_out[:, chunks[layer], :] = full[:, chunks[layer], :]


def shards(
    features, spacing, targets, ray_length, cell_id, slot_rank, image_id,
    params, first_moment, second_moment, code_table, table_first, table_second,
):
    ray_rows = features.shape[0]
    sample_count = ray_rows * SAMPLES
    groups = lax.axis_size("expert")
    experts_all = params.shape[0] * groups
    cap = 2 * (sample_count * 3 // 4 // experts_all)
    cap_up = -(-cap // LANES) * LANES
    width = cap_up + LANES
    slots_up = experts_all * cap_up
    table_rows = code_table.shape[0]
    block_index = lax.axis_index("expert") * lax.axis_size("dp") + lax.axis_index("dp")
    local_image = (image_id - block_index * table_rows)[None, :]
    cell = cell_id.T
    rank = slot_rank.T
    slot = jnp.where(rank >= 0, cell * cap_up + rank, slots_up).reshape(sample_count)
    weights_bf = params.astype(BF16)
    queries = weights_bf[:, HEAD_ROW + 4 : HEAD_ROW + 8, :CODE_WIDTH].reshape(8, CODE_WIDTH)
    shift = weights_bf[:, HEAD_ROW + 8, :4].reshape(8, 1)
    tail_msg = jnp.pad(
        jnp.concatenate([queries, shift], axis=1).astype(F32),
        ((0, 0), (0, LANES - CODE_WIDTH - 1)),
    )
    shape = jax.ShapeDtypeStruct
    big = 60 * 2**20
    table_scratch = pltpu.VMEM((slots_up + 8, LANES), F32)
    rows_scratch = pltpu.VMEM((sample_count, LANES), F32)
    msg_shape = (groups, 8, width)
    disp = pl.pallas_call(
        functools.partial(place_kernel, groups, cap, cap_up),
        out_shape=shape((groups, cap, LANES), BF16),
        in_specs=[SMEM, VMEM],
        out_specs=VMEM,
        scratch_shapes=[rows_scratch, table_scratch],
        compiler_params=pltpu.CompilerParams(vmem_limit_bytes=32 * 2**20),
        name="place",
    )(slot, features.transpose(1, 2, 0))
    sems = pltpu.SemaphoreType.DMA((groups,))
    arr, raw_back = pl.pallas_call(
        functools.partial(forward_kernel, groups, cap, cap_up),
        out_shape=(shape((groups, cap, LANES), BF16), shape(msg_shape, F32)),
        in_specs=[VMEM] * 3,
        out_specs=(VMEM, VMEM),
        scratch_shapes=[
            pltpu.VMEM((groups, cap, LANES), BF16),
            pltpu.VMEM(msg_shape, F32),
            pltpu.VMEM(msg_shape, F32),
            pltpu.VMEM((2, LANES, NET_WIDTH), BF16),
            sems, sems, sems, sems,
        ],
        compiler_params=pltpu.CompilerParams(
            collective_id=0, has_side_effects=True, vmem_limit_bytes=32 * 2**20
        ),
        name="dispatch",
    )(disp, weights_bf, tail_msg)
    table_shape = shape(code_table.shape, F32)
    loss, cot_msg, new_table, new_table_first, new_table_second = pl.pallas_call(
        functools.partial(home_kernel, groups, cap_up),
        out_shape=(
            shape((1, ray_rows), F32), shape(msg_shape, F32), table_shape, table_shape, table_shape,
        ),
        in_specs=[SMEM] + [VMEM] * 9,
        out_specs=(VMEM,) * 5,
        scratch_shapes=[
            rows_scratch,
            table_scratch,
            pltpu.VMEM((8 * SAMPLES, LANES), F32),
            pltpu.VMEM((8 * groups, LANES), F32),
            pltpu.VMEM((8 * groups, CODE_WIDTH), F32),
            pltpu.VMEM((8 * groups, LANES), F32),
        ],
        compiler_params=pltpu.CompilerParams(vmem_limit_bytes=32 * 2**20),
        name="home",
    )(
        slot, raw_back, cell, spacing.T, ray_length[None, :], targets, local_image,
        code_table, table_first, table_second,
    )
    all_rows = groups * cap
    grad_rows = params.shape[1]
    param_grad = pl.pallas_call(
        functools.partial(backward_kernel, groups, cap, cap_up),
        out_shape=shape(params.shape, F32),
        in_specs=[VMEM] * 3,
        out_specs=VMEM,
        scratch_shapes=[
            pltpu.VMEM(msg_shape, F32),
            pltpu.VMEM((LAYERS, 2, all_rows, NET_WIDTH), BF16),
            pltpu.VMEM((LAYERS, 2, all_rows, NET_WIDTH), BF16),
            pltpu.VMEM((2, LANES, NET_WIDTH), BF16),
            pltpu.VMEM((2, 8, NET_WIDTH), F32),
            pltpu.VMEM((8, LANES), F32),
            pltpu.VMEM((8, LANES), F32),
            pltpu.VMEM((2, grad_rows, NET_WIDTH), F32),
            pltpu.VMEM((grad_rows, NET_WIDTH), F32),
            pltpu.VMEM((grad_rows, NET_WIDTH), BF16),
            pltpu.VMEM((grad_rows, NET_WIDTH), BF16),
            pltpu.VMEM((2, grad_rows, NET_WIDTH), F32),
            sems, sems,
            pltpu.SemaphoreType.DMA((3, LAYERS)),
            pltpu.SemaphoreType.DMA((3, LAYERS)),
        ],
        compiler_params=pltpu.CompilerParams(
            collective_id=1, has_side_effects=True, vmem_limit_bytes=big
        ),
        name="backward",
    )(cot_msg, weights_bf, arr.reshape(all_rows, LANES))
    new_params, new_first, new_second = adam_update(params, param_grad, first_moment, second_moment)
    return (
        loss.reshape(ray_rows), new_params, new_first, new_second,
        new_table, new_table_first, new_table_second,
    )


def solution(mesh):
    both = ("expert", "dp")
    return jax.shard_map(
        shards,
        mesh=mesh,
        in_specs=(
            P(both, None, None), P(both, None), P(None, both), P(both), P(both, None),
            P(both, None), P(both),
            P("expert", None, None), P("expert", None, None), P("expert", None, None),
            P(both, None), P(both, None), P(both, None),
        ),
        out_specs=(
            P(both),
            P("expert", None, None), P("expert", None, None), P("expert", None, None),
            P(both, None), P(both, None), P(both, None),
        ),
        check_vma=False,
    )
```

```python
import functools

import jax
import jax.numpy as jnp
from jax import lax
from jax.experimental import pallas as pl
from jax.experimental.pallas import tpu as pltpu
from jax.sharding import PartitionSpec as P

NET_WIDTH = 256
CODE_WIDTH = 64
ENC_WIDTH = 64
LAYERS = 4
SAMPLES = 32
HEAD_ROW = ENC_WIDTH + (LAYERS - 1) * NET_WIDTH
LANES = 128

BETA_ONE = 0.9
BETA_TWO = 0.999
LEARN_RATE = 0.001
ADAM_EPS = 1e-08
CORRECT_ONE = 1.0 - 0.9**10
CORRECT_TWO = 1.0 - 0.999**10

MESH = pl.DeviceIdType.MESH
VMEM = pl.BlockSpec(memory_space=pltpu.VMEM)
SMEM = pl.BlockSpec(memory_space=pltpu.SMEM)
F32 = jnp.float32
BF16 = jnp.bfloat16
NN = (((1,), (0,)), ((), ()))
NT = (((1,), (1,)), ((), ()))
TN = (((0,), (0,)), ((), ()))


def dot(left, right, dims=NN, precision=None):
    return lax.dot_general(left, right, dims, precision=precision, preferred_element_type=F32)


def exact(left, right, dims=NN):
    return dot(left, right, dims, lax.Precision.HIGHEST)


def adam_update(param_now, gradient, moment_one, moment_two):
    new_one = BETA_ONE * moment_one + (1.0 - BETA_ONE) * gradient
    new_two = BETA_TWO * moment_two + (1.0 - BETA_TWO) * gradient * gradient
    update = LEARN_RATE * (new_one / CORRECT_ONE) / (jnp.sqrt(new_two / CORRECT_TWO) + ADAM_EPS)
    return (param_now - update, new_one, new_two)


def lane_block(index):
    return pl.ds(pl.multiple_of(index * LANES, LANES), LANES)


def move_rows(count, move):
    step = 32

    def body(block, carry):
        for inner in range(step):
            move(block * step + inner)
        return carry

    lax.fori_loop(0, count // step, body, 0)


def place_kernel(groups, cap, cap_up, slot_ref, feat_ref, out_ref, rows, table):
    table[...] = jnp.zeros_like(table)

    def turn(i, carry):
        block = feat_ref[i].astype(F32)
        rows[lane_block(i), :] = jnp.concatenate([block, block], axis=0).T
        return carry

    lax.fori_loop(0, SAMPLES, turn, 0)

    def move(s):
        table[pl.ds(slot_ref[s], 1), :] = rows[pl.ds(s, 1), :]

    move_rows(rows.shape[0], move)
    low = lax.broadcasted_iota(jnp.int32, (cap, LANES), 1) < ENC_WIDTH

    def pack(g, carry):
        first = table[pl.ds(pl.multiple_of(2 * g * cap_up, LANES), cap), :]
        second = table[pl.ds(pl.multiple_of((2 * g + 1) * cap_up, LANES), cap), :]
        out_ref[g] = jnp.where(low, first, second).astype(BF16)
        return carry

    lax.fori_loop(0, groups, pack, 0)


def greet(groups, me):
    barrier = pltpu.get_barrier_semaphore()

    def body(k, carry):
        pl.semaphore_signal(
            barrier, 1, device_id={"expert": lax.rem(me + k, groups)}, device_id_type=MESH
        )
        return carry

    lax.fori_loop(1, groups, body, 0)
    return barrier


def pad_first(wt_ref, m0):
    m0[...] = jnp.zeros_like(m0)
    for h in range(2):
        m0[h, ENC_WIDTH * h : ENC_WIDTH * (h + 1), :] = wt_ref[h, 0:ENC_WIDTH, :]


def layer_matrix(wt_ref, m0, h, layer):
    if layer == 0:
        return m0[h]
    start = ENC_WIDTH + (layer - 1) * NET_WIDTH
    return wt_ref[h, start : start + NET_WIDTH, :]


def tail_rows(wt_ref, h):
    return wt_ref[h, HEAD_ROW : HEAD_ROW + 16, :]


def forward(wt_ref, m0, block, keep=None):
    tails = [tail_rows(wt_ref, h).astype(F32) for h in range(2)]
    current = [block, block]
    for layer in range(LAYERS):
        for h in range(2):
            preact = dot(current[h], layer_matrix(wt_ref, m0, h, layer))
            preact = preact + tails[h][9 + layer : 10 + layer, :]
            current[h] = jnp.maximum(preact, 0.0).astype(BF16)
            if keep is not None:
                keep(layer, h, current[h])
    return current


def forward_kernel(
    groups, cap, cap_up, disp, params, arr, raw_out, wt, recv, msg, back, m0, tail_msg,
    s1, r1, s2, r2,
):
    me = lax.axis_index("expert")
    barrier = greet(groups, me)
    pl.semaphore_wait(barrier, groups - 1)

    def out_copy(k):
        peer = lax.rem(me + k, groups)
        return pltpu.make_async_remote_copy(
            disp.at[peer], recv.at[k], s1.at[k], r1.at[k],
            device_id={"expert": peer}, device_id_type=MESH,
        )

    def back_copy(k):
        peer = lax.rem(me + groups - k, groups)
        return pltpu.make_async_remote_copy(
            msg.at[k], back.at[me], s2.at[k], r2.at[k],
            device_id={"expert": peer}, device_id_type=MESH,
        )

    def start(k, carry):
        out_copy(k).start()
        return carry

    lax.fori_loop(1, groups, start, 0)
    wt[...] = params[...].astype(BF16)
    pad_first(wt, m0)
    spot = lax.broadcasted_iota(jnp.int32, (4, LANES), 0) == lax.broadcasted_iota(
        jnp.int32, (4, LANES), 1
    )
    lane = lax.broadcasted_iota(jnp.int32, (4, LANES), 1)
    for h in range(2):
        tail = tail_rows(wt, h).astype(F32)
        column = jnp.sum(jnp.where(spot, tail[8:9, 0:LANES], 0.0), axis=1, keepdims=True)
        tail_msg[4 * h : 4 * h + 4, :] = jnp.where(
            lane < CODE_WIDTH, tail[4:8, 0:LANES], jnp.where(lane == CODE_WIDTH, column, 0.0)
        )

    def process(k, block):
        arr[k] = block
        msg[k, :, cap_up:] = tail_msg[...]
        if cap_up > cap:
            msg[k, :, cap:cap_up] = jnp.zeros((8, cap_up - cap), F32)
        acts = forward(wt, m0, block)
        for h in range(2):
            raw = dot(tail_rows(wt, h), acts[h], NT)
            msg[k, 4 * h : 4 * h + 4, 0:cap] = raw[0:4]

    process(0, disp[me])
    back[me] = msg[0]

    def step(k, carry):
        out_copy(k).wait_recv()
        process(k, recv[k])
        back_copy(k).start()
        return carry

    lax.fori_loop(1, groups, step, 0)

    def finish(k, carry):
        out_copy(k).wait_send()
        back_copy(k).wait_send()
        back_copy(k).wait_recv()
        return carry

    lax.fori_loop(1, groups, finish, 0)
    raw_out[...] = back[...]


def home_kernel(
    groups, cap_up, slot_ref, raw_ref, cell_ref, spacing_ref, length_ref, target_ref, image_ref,
    code_ref, first_ref, second_ref, loss_out, msg_out, code_out, first_out, second_out,
    rows, table, eight, mix, queries, shift,
):
    tiles = cap_up // LANES
    filler = jnp.zeros((LANES - 8, LANES), F32)

    def widen(g, carry):
        for t in range(tiles):
            piece = raw_ref[g, :, t * LANES : (t + 1) * LANES]
            turned = jnp.concatenate([piece, filler], axis=0).T
            for h in range(2):
                start = pl.multiple_of((2 * g + h) * cap_up + t * LANES, LANES)
                table[pl.ds(start, LANES), :] = turned
        block = pl.ds(pl.multiple_of(8 * g, 8), 8)
        queries[block, :] = raw_ref[g, :, cap_up : cap_up + CODE_WIDTH]
        shift[block, :] = jnp.broadcast_to(
            raw_ref[g, :, cap_up + CODE_WIDTH : cap_up + CODE_WIDTH + 1], (8, LANES)
        )
        return carry

    lax.fori_loop(0, groups, widen, 0)
    table[pl.ds(2 * groups * cap_up, 8), :] = jnp.zeros((8, LANES), F32)

    def take(s):
        rows[pl.ds(s, 1), :] = table[pl.ds(slot_ref[s], 1), :]

    move_rows(rows.shape[0], take)

    def narrow(i, carry):
        eight[pl.ds(pl.multiple_of(8 * i, 8), 8), :] = rows[lane_block(i), :].T[0:8]
        return carry

    lax.fori_loop(0, SAMPLES, narrow, 0)
    table[...] = jnp.zeros_like(table)

    table_rows = code_ref.shape[0]
    pick = (
        lax.broadcasted_iota(jnp.int32, (table_rows, LANES), 0) == image_ref[...]
    ).astype(F32)
    code_bf = code_ref[...].astype(BF16).astype(F32)
    ray_code = exact(code_bf, pick, TN)
    mix[...] = exact(queries[...], ray_code) + shift[...]

    cell = cell_ref[...]
    odd = lax.rem(cell, 2) == 1
    row = lax.broadcasted_iota(jnp.int32, (SAMPLES, LANES), 0)
    live = row < length_ref[...]
    raws = tuple(
        jnp.where(
            odd, eight[pl.ds(4 + c, SAMPLES, 8), :], eight[pl.ds(c, SAMPLES, 8), :]
        )
        for c in range(4)
    )

    def add_code(g, raws):
        part = mix[pl.ds(pl.multiple_of(8 * g, 8), 8), :]
        raws = list(raws)
        for h in range(2):
            hit = cell == 2 * g + h
            for c in range(4):
                j = 4 * h + c
                raws[c] = raws[c] + jnp.where(hit, part[j : j + 1, :], 0.0)
        return tuple(raws)

    raws = lax.fori_loop(0, groups, add_code, raws)
    raws = [jnp.where(live, raw, 0.0) for raw in raws]
    spacing = spacing_ref[...]
    density = jnp.maximum(raws[0], 0.0) + jnp.log1p(jnp.exp(-jnp.abs(raws[0])))
    colors = [jax.nn.sigmoid(raw) for raw in raws[1:]]
    tau = jnp.where(live, density * spacing, 0.0)
    square_row = lax.broadcasted_iota(jnp.int32, (SAMPLES, SAMPLES), 0)
    square_col = lax.broadcasted_iota(jnp.int32, (SAMPLES, SAMPLES), 1)
    before = exact((square_col < square_row).astype(F32), tau)
    through = jnp.exp(-before)
    fade = jnp.exp(-tau)
    weight = through * (1.0 - fade)
    gaps = [
        jnp.sum(weight * colors[c], axis=0, keepdims=True) - target_ref[c : c + 1, :]
        for c in range(3)
    ]
    loss_out[...] = 0.5 * (gaps[0] * gaps[0] + gaps[1] * gaps[1] + gaps[2] * gaps[2])
    pull = gaps[0] * colors[0] + gaps[1] * colors[1] + gaps[2] * colors[2]
    after = exact((square_col > square_row).astype(F32), pull * weight)
    tau_grad = pull * through * fade - after
    grads = [tau_grad * spacing * jax.nn.sigmoid(raws[0])]
    for c in range(3):
        grads.append(gaps[c] * weight * colors[c] * (1.0 - colors[c]))
    cots = [jnp.where(live, grad, 0.0).astype(BF16).astype(F32) for grad in grads]
    for c in range(4):
        eight[pl.ds(c, SAMPLES, 8), :] = jnp.where(odd, 0.0, cots[c])
        eight[pl.ds(4 + c, SAMPLES, 8), :] = jnp.where(odd, cots[c], 0.0)

    def gather_code(g, carry):
        pieces = []
        for h in range(2):
            hit = cell == 2 * g + h
            for c in range(4):
                pieces.append(jnp.sum(jnp.where(hit, cots[c], 0.0), axis=0, keepdims=True))
        mix[pl.ds(pl.multiple_of(8 * g, 8), 8), :] = jnp.concatenate(pieces, axis=0)
        return carry

    lax.fori_loop(0, groups, gather_code, 0)
    totals = mix[...]
    query_grad = exact(totals, ray_code, NT)
    table_grad = exact(exact(totals, pick, NT), queries[...], TN)
    new_code, new_first, new_second = adam_update(
        code_ref[...], table_grad, first_ref[...], second_ref[...]
    )
    code_out[...] = new_code
    first_out[...] = new_first
    second_out[...] = new_second
    queries[...] = query_grad

    def widen_back(i, carry):
        piece = eight[pl.ds(pl.multiple_of(8 * i, 8), 8), :]
        rows[lane_block(i), :] = jnp.concatenate([piece, filler], axis=0).T
        return carry

    lax.fori_loop(0, SAMPLES, widen_back, 0)

    def put(s):
        table[pl.ds(slot_ref[s], 1), :] = rows[pl.ds(s, 1), :]

    move_rows(rows.shape[0], put)

    def pack(g, carry):
        for t in range(tiles):
            start = [pl.multiple_of((2 * g + h) * cap_up + t * LANES, LANES) for h in range(2)]
            both = table[pl.ds(start[0], LANES), :] + table[pl.ds(start[1], LANES), :]
            msg_out[g, :, t * LANES : (t + 1) * LANES] = both.T[0:8]
        part = queries[pl.ds(pl.multiple_of(8 * g, 8), 8), :]
        msg_out[g, :, cap_up:] = jnp.concatenate(
            [part, jnp.zeros((8, LANES - CODE_WIDTH), F32)], axis=1
        )
        return carry

    lax.fori_loop(0, groups, pack, 0)


def backward_kernel(
    groups, cap, cap_up, msg, wt, arr, grad_out, recv, act, pre, m0, turned, head, code_sum,
    cot_sum, bias, grad, half_in, sum_out, sum_in, full, s1, r1, s2, r2,
):
    me = lax.axis_index("expert")
    my_dp = lax.axis_index("dp")
    core = lax.rem(my_dp, 2)
    near = my_dp + 1 - 2 * core
    far = my_dp + 2 - 4 * lax.rem(my_dp // 2, 2)
    barrier = greet(groups, me)
    for peer in (near, far):
        pl.semaphore_signal(barrier, 1, device_id={"dp": peer}, device_id_type=MESH)
    pl.semaphore_wait(barrier, groups + 1)

    def out_copy(k):
        peer = lax.rem(me + k, groups)
        return pltpu.make_async_remote_copy(
            msg.at[peer], recv.at[k], s1.at[k], r1.at[k],
            device_id={"expert": peer}, device_id_type=MESH,
        )

    def start(k, carry):
        out_copy(k).start()
        return carry

    lax.fori_loop(1, groups, start, 0)
    pad_first(wt, m0)
    head[...] = jnp.zeros_like(head)
    bias[...] = jnp.zeros_like(bias)
    for h in range(2):
        head[h, 4 * h : 4 * h + 4, :] = tail_rows(wt, h).astype(F32)[0:4]
        for layer in range(1, LAYERS):
            matrix = layer_matrix(wt, m0, h, layer)
            turned[layer - 1, h] = matrix.astype(F32).T.astype(BF16)

    pieces = 4
    size = arr.shape[0] // pieces

    def piece(index):
        return pl.ds(pl.multiple_of(index * size, 16), size)

    def again(index, carry):
        block = piece(index)

        def keep(layer, h, value):
            act[layer, h, block, :] = value

        forward(wt, m0, arr[block, :], keep)
        return carry

    lax.fori_loop(0, pieces, again, 0)
    recv[0] = msg[me]

    def arrive(k, carry):
        out_copy(k).wait()
        return carry

    lax.fori_loop(1, groups, arrive, 0)

    starts = [0] + [ENC_WIDTH + layer * NET_WIDTH for layer in range(LAYERS)] + [HEAD_ROW + 16]
    chunks = [pl.ds(starts[j], starts[j + 1] - starts[j]) for j in range(LAYERS + 1)]

    def near_copy(j):
        return pltpu.make_async_remote_copy(
            grad.at[1 - core, chunks[j]], half_in.at[chunks[j]],
            s2.at[0, j], r2.at[0, j], device_id={"dp": near}, device_id_type=MESH,
        )

    def far_copy(j):
        return pltpu.make_async_remote_copy(
            sum_out.at[chunks[j]], sum_in.at[chunks[j]],
            s2.at[1, j], r2.at[1, j], device_id={"dp": far}, device_id_type=MESH,
        )

    def full_copy(j, which):
        return pltpu.make_async_remote_copy(
            full.at[which, chunks[j]], full.at[which, chunks[j]],
            s2.at[2, j], r2.at[2, j], device_id={"dp": near}, device_id_type=MESH,
        )

    def second_stage(j):
        near_copy(j).wait_recv()
        rows = chunks[j]
        sum_out[rows, :] = (grad[core, rows, :] + half_in[rows, :]).astype(BF16)
        far_copy(j).start()

    def third_stage(j):
        far_copy(j).wait_recv()
        rows = chunks[j]
        full[core, rows, :] = sum_out[rows, :].astype(F32) + sum_in[rows, :].astype(F32)
        full_copy(j, core).start()

    top = LAYERS - 1
    heads_bf = [head[h].astype(BF16) for h in range(2)]

    def mask_store(layer, h, block, up):
        value = jnp.where(act[layer, h, block, :].astype(F32) > 0, up, 0.0).astype(BF16)
        pre[layer, h, block, :] = value
        bias[layer, h] += jnp.sum(
            value.astype(F32).reshape(-1, 8, NET_WIDTH), axis=0
        )

    code_sum[...] = jnp.zeros_like(code_sum)
    cot_sum[...] = jnp.zeros_like(cot_sum)

    def first_back(k, carry):
        block = pl.ds(pl.multiple_of(k * cap, 16), cap)
        cot = recv[k, :, 0:cap].astype(BF16)
        sums = []
        for h in range(2):
            mask_store(top, h, block, dot(cot, heads_bf[h], TN))
            sums.append(carry[h] + dot(cot, act[top, h, block, :]))
        code_sum[...] += recv[k, :, cap_up:]
        cot_sum[...] += jnp.broadcast_to(
            jnp.sum(recv[k, :, 0:cap], axis=1, keepdims=True), (8, LANES)
        )
        return tuple(sums)

    hidden = lax.fori_loop(
        0, groups, first_back, (jnp.zeros((8, NET_WIDTH), F32), jnp.zeros((8, NET_WIDTH), F32))
    )

    for layer in reversed(range(LAYERS)):
        if layer < top:

            def back(index, carry):
                block = piece(index)
                for h in range(2):
                    mask_store(
                        layer, h, block, dot(pre[layer + 1, h, block, :], turned[layer, h])
                    )
                return carry

            lax.fori_loop(0, pieces, back, 0)
        for h in range(2):
            if layer == 0:
                value = dot(arr[...], pre[0, h], TN)
                grad[h, 0:ENC_WIDTH, :] = value[ENC_WIDTH * h : ENC_WIDTH * (h + 1)]
            else:
                grad[h, chunks[layer], :] = dot(act[layer - 1, h], pre[layer, h], TN)
        near_copy(layer).start()
        if layer < top:
            second_stage(layer + 1)
        if layer < top - 1:
            third_stage(layer + 2)

    codes = jnp.concatenate([code_sum[...], jnp.zeros((8, NET_WIDTH - LANES), F32)], axis=1)
    spot = (
        lax.broadcasted_iota(jnp.int32, (8, LANES), 0)
        == lax.broadcasted_iota(jnp.int32, (8, LANES), 1)
    )
    cot_row = jnp.sum(jnp.where(spot, cot_sum[...], 0.0), axis=0, keepdims=True)
    lane = lax.broadcasted_iota(jnp.int32, (1, LANES), 1)
    for h in range(2):
        line = cot_row if h == 0 else pltpu.roll(cot_row, LANES - 4, 1)
        line = jnp.where(lane < 4, line, 0.0)
        line = jnp.concatenate([line, jnp.zeros((1, NET_WIDTH - LANES), F32)], axis=1)
        grad[h, HEAD_ROW : HEAD_ROW + 16, :] = jnp.concatenate(
            [hidden[h][4 * h : 4 * h + 4], codes[4 * h : 4 * h + 4], line]
            + [jnp.sum(bias[layer, h], axis=0, keepdims=True) for layer in range(LAYERS)]
            + [jnp.zeros((7 - LAYERS, NET_WIDTH), F32)],
            axis=0,
        )
    near_copy(LAYERS).start()
    second_stage(0)
    third_stage(1)
    second_stage(LAYERS)
    third_stage(0)
    third_stage(LAYERS)
    for j in (3, 2, 1, 0, LAYERS):
        near_copy(j).wait_send()
        far_copy(j).wait_send()
        full_copy(j, core).wait_send()
        full_copy(j, 1 - core).wait_recv()
        grad_out[:, chunks[j], :] = full[:, chunks[j], :]


def shards(
    features, spacing, targets, ray_length, cell_id, slot_rank, image_id,
    params, first_moment, second_moment, code_table, table_first, table_second,
):
    ray_rows = features.shape[0]
    sample_count = ray_rows * SAMPLES
    groups = lax.axis_size("expert")
    experts_all = params.shape[0] * groups
    cap = 2 * (sample_count * 3 // 4 // experts_all)
    cap_up = -(-cap // LANES) * LANES
    width = cap_up + LANES
    slots_up = experts_all * cap_up
    table_rows = code_table.shape[0]
    block_index = lax.axis_index("expert") * lax.axis_size("dp") + lax.axis_index("dp")
    local_image = (image_id - block_index * table_rows)[None, :]
    cell = cell_id.T
    rank = slot_rank.T
    slot = jnp.where(rank >= 0, cell * cap_up + rank, slots_up).reshape(sample_count)
    shape = jax.ShapeDtypeStruct
    big = 46 * 2**20
    table_scratch = pltpu.VMEM((slots_up + 8, LANES), F32)
    rows_scratch = pltpu.VMEM((sample_count, LANES), F32)
    msg_shape = (groups, 8, width)
    disp = pl.pallas_call(
        functools.partial(place_kernel, groups, cap, cap_up),
        out_shape=shape((groups, cap, LANES), BF16),
        in_specs=[SMEM, VMEM],
        out_specs=VMEM,
        scratch_shapes=[rows_scratch, table_scratch],
        compiler_params=pltpu.CompilerParams(vmem_limit_bytes=32 * 2**20),
        name="place",
    )(slot, features.transpose(1, 2, 0))
    sems = pltpu.SemaphoreType.DMA((groups,))
    arr, raw_back, weights_bf = pl.pallas_call(
        functools.partial(forward_kernel, groups, cap, cap_up),
        out_shape=(
            shape((groups, cap, LANES), BF16), shape(msg_shape, F32), shape(params.shape, BF16),
        ),
        in_specs=[VMEM] * 2,
        out_specs=(VMEM,) * 3,
        scratch_shapes=[
            pltpu.VMEM((groups, cap, LANES), BF16),
            pltpu.VMEM(msg_shape, F32),
            pltpu.VMEM(msg_shape, F32),
            pltpu.VMEM((2, LANES, NET_WIDTH), BF16),
            pltpu.VMEM((8, LANES), F32),
            sems, sems, sems, sems,
        ],
        compiler_params=pltpu.CompilerParams(
            collective_id=0, has_side_effects=True, vmem_limit_bytes=32 * 2**20
        ),
        name="dispatch",
    )(disp, params)
    table_shape = shape(code_table.shape, F32)
    loss, cot_msg, new_table, new_table_first, new_table_second = pl.pallas_call(
        functools.partial(home_kernel, groups, cap_up),
        out_shape=(
            shape((1, ray_rows), F32), shape(msg_shape, F32), table_shape, table_shape, table_shape,
        ),
        in_specs=[SMEM] + [VMEM] * 9,
        out_specs=(VMEM,) * 5,
        scratch_shapes=[
            rows_scratch,
            table_scratch,
            pltpu.VMEM((8 * SAMPLES, LANES), F32),
            pltpu.VMEM((8 * groups, LANES), F32),
            pltpu.VMEM((8 * groups, CODE_WIDTH), F32),
            pltpu.VMEM((8 * groups, LANES), F32),
        ],
        compiler_params=pltpu.CompilerParams(vmem_limit_bytes=32 * 2**20),
        name="home",
    )(
        slot, raw_back, cell, spacing.T, ray_length[None, :], targets, local_image,
        code_table, table_first, table_second,
    )
    all_rows = groups * cap
    grad_rows = params.shape[1]
    param_grad = pl.pallas_call(
        functools.partial(backward_kernel, groups, cap, cap_up),
        out_shape=shape(params.shape, F32),
        in_specs=[VMEM] * 3,
        out_specs=VMEM,
        scratch_shapes=[
            pltpu.VMEM(msg_shape, F32),
            pltpu.VMEM((LAYERS, 2, all_rows, NET_WIDTH), BF16),
            pltpu.VMEM((LAYERS, 2, all_rows, NET_WIDTH), BF16),
            pltpu.VMEM((2, LANES, NET_WIDTH), BF16),
            pltpu.VMEM((LAYERS - 1, 2, NET_WIDTH, NET_WIDTH), BF16),
            pltpu.VMEM((2, 8, NET_WIDTH), F32),
            pltpu.VMEM((8, LANES), F32),
            pltpu.VMEM((8, LANES), F32),
            pltpu.VMEM((LAYERS, 2, 8, NET_WIDTH), F32),
            pltpu.VMEM((2, grad_rows, NET_WIDTH), F32),
            pltpu.VMEM((grad_rows, NET_WIDTH), F32),
            pltpu.VMEM((grad_rows, NET_WIDTH), BF16),
            pltpu.VMEM((grad_rows, NET_WIDTH), BF16),
            pltpu.VMEM((2, grad_rows, NET_WIDTH), F32),
            sems, sems,
            pltpu.SemaphoreType.DMA((3, LAYERS + 1)),
            pltpu.SemaphoreType.DMA((3, LAYERS + 1)),
        ],
        compiler_params=pltpu.CompilerParams(
            collective_id=1, has_side_effects=True, vmem_limit_bytes=big
        ),
        name="backward",
    )(cot_msg, weights_bf, arr.reshape(all_rows, LANES))
    new_params, new_first, new_second = adam_update(params, param_grad, first_moment, second_moment)
    return (
        loss.reshape(ray_rows), new_params, new_first, new_second,
        new_table, new_table_first, new_table_second,
    )


def solution(mesh):
    both = ("expert", "dp")
    return jax.shard_map(
        shards,
        mesh=mesh,
        in_specs=(
            P(both, None, None), P(both, None), P(None, both), P(both), P(both, None),
            P(both, None), P(both),
            P("expert", None, None), P("expert", None, None), P("expert", None, None),
            P(both, None), P(both, None), P(both, None),
        ),
        out_specs=(
            P(both),
            P("expert", None, None), P("expert", None, None), P("expert", None, None),
            P(both, None), P(both, None), P(both, None),
        ),
        check_vma=False,
    )
```

```python
import functools

import jax
import jax.numpy as jnp
from jax import lax
from jax.experimental import pallas as pl
from jax.experimental.pallas import tpu as pltpu
from jax.sharding import PartitionSpec as P

NET_WIDTH = 256
CODE_WIDTH = 64
ENC_WIDTH = 64
LAYERS = 4
SAMPLES = 32
HEAD_ROW = ENC_WIDTH + (LAYERS - 1) * NET_WIDTH
LANES = 128

BETA_ONE = 0.9
BETA_TWO = 0.999
LEARN_RATE = 0.001
ADAM_EPS = 1e-08
CORRECT_ONE = 1.0 - 0.9**10
CORRECT_TWO = 1.0 - 0.999**10

MESH = pl.DeviceIdType.MESH
VMEM = pl.BlockSpec(memory_space=pltpu.VMEM)
SMEM = pl.BlockSpec(memory_space=pltpu.SMEM)
F32 = jnp.float32
BF16 = jnp.bfloat16
NN = (((1,), (0,)), ((), ()))
NT = (((1,), (1,)), ((), ()))
TN = (((0,), (0,)), ((), ()))


def dot(left, right, dims=NN, precision=None):
    return lax.dot_general(left, right, dims, precision=precision, preferred_element_type=F32)


def exact(left, right, dims=NN):
    return dot(left, right, dims, lax.Precision.HIGHEST)


def adam_update(param_now, gradient, moment_one, moment_two):
    new_one = BETA_ONE * moment_one + (1.0 - BETA_ONE) * gradient
    new_two = BETA_TWO * moment_two + (1.0 - BETA_TWO) * gradient * gradient
    update = LEARN_RATE * (new_one / CORRECT_ONE) / (jnp.sqrt(new_two / CORRECT_TWO) + ADAM_EPS)
    return (param_now - update, new_one, new_two)


def lane_block(index):
    return pl.ds(pl.multiple_of(index * LANES, LANES), LANES)


def move_rows(count, move):
    step = 128

    def body(block, carry):
        for inner in range(step):
            move(block * step + inner)
        return carry

    lax.fori_loop(0, count // step, body, 0)


def unrolled(count, body, step=4):
    def several(index, carry):
        for inner in range(step):
            body(index * step + inner)
        return carry

    lax.fori_loop(0, count // step, several, 0)


def place_kernel(groups, cap, cap_up, slot_ref, feat_ref, out_ref, rows, table):
    table[...] = jnp.zeros_like(table)

    def turn(i):
        block = feat_ref[i].astype(F32)
        rows[lane_block(i), :] = jnp.concatenate([block, block], axis=0).T

    unrolled(SAMPLES, turn)

    def move(s):
        table[pl.ds(slot_ref[s], 1), :] = rows[pl.ds(s, 1), :]

    move_rows(rows.shape[0], move)
    low = lax.broadcasted_iota(jnp.int32, (cap, LANES), 1) < ENC_WIDTH

    def pack(g, carry):
        first = table[pl.ds(pl.multiple_of(2 * g * cap_up, LANES), cap), :]
        second = table[pl.ds(pl.multiple_of((2 * g + 1) * cap_up, LANES), cap), :]
        out_ref[g] = jnp.where(low, first, second).astype(BF16)
        return carry

    lax.fori_loop(0, groups, pack, 0)


def greet(groups, me):
    barrier = pltpu.get_barrier_semaphore()

    def body(k, carry):
        pl.semaphore_signal(
            barrier, 1, device_id={"expert": lax.rem(me + k, groups)}, device_id_type=MESH
        )
        return carry

    lax.fori_loop(1, groups, body, 0)
    return barrier


def pad_first(wt_ref, m0):
    m0[...] = jnp.zeros_like(m0)
    for h in range(2):
        m0[h, ENC_WIDTH * h : ENC_WIDTH * (h + 1), :] = wt_ref[h, 0:ENC_WIDTH, :]


def layer_matrix(wt_ref, m0, h, layer):
    if layer == 0:
        return m0[h]
    start = ENC_WIDTH + (layer - 1) * NET_WIDTH
    return wt_ref[h, start : start + NET_WIDTH, :]


def tail_rows(wt_ref, h):
    return wt_ref[h, HEAD_ROW : HEAD_ROW + 16, :]


def forward(wt_ref, m0, block, keep=None):
    tails = [tail_rows(wt_ref, h).astype(F32) for h in range(2)]
    current = [block, block]
    for layer in range(LAYERS):
        for h in range(2):
            preact = dot(current[h], layer_matrix(wt_ref, m0, h, layer))
            preact = preact + tails[h][9 + layer : 10 + layer, :]
            current[h] = jnp.maximum(preact, 0.0).astype(BF16)
            if keep is not None:
                keep(layer, h, current[h])
    return current


def forward_kernel(
    groups, cap, cap_up, disp, params, arr, raw_out, wt, recv, msg, back, m0, tail_msg,
    master, master_sem, s1, r1, s2, r2,
):
    me = lax.axis_index("expert")
    load = pltpu.make_async_copy(params, master, master_sem)
    load.start()
    barrier = greet(groups, me)
    pl.semaphore_wait(barrier, groups - 1)

    def out_copy(k):
        peer = lax.rem(me + k, groups)
        return pltpu.make_async_remote_copy(
            disp.at[peer], recv.at[k], s1.at[k], r1.at[k],
            device_id={"expert": peer}, device_id_type=MESH,
        )

    def back_copy(k):
        peer = lax.rem(me + groups - k, groups)
        return pltpu.make_async_remote_copy(
            msg.at[k], back.at[me], s2.at[k], r2.at[k],
            device_id={"expert": peer}, device_id_type=MESH,
        )

    def start(k, carry):
        out_copy(k).start()
        return carry

    lax.fori_loop(1, groups, start, 0)
    load.wait()
    wt[...] = master[...].astype(BF16)
    pad_first(wt, m0)
    spot = lax.broadcasted_iota(jnp.int32, (4, LANES), 0) == lax.broadcasted_iota(
        jnp.int32, (4, LANES), 1
    )
    lane = lax.broadcasted_iota(jnp.int32, (4, LANES), 1)
    for h in range(2):
        tail = tail_rows(wt, h).astype(F32)
        column = jnp.sum(jnp.where(spot, tail[8:9, 0:LANES], 0.0), axis=1, keepdims=True)
        tail_msg[4 * h : 4 * h + 4, :] = jnp.where(
            lane < CODE_WIDTH, tail[4:8, 0:LANES], jnp.where(lane == CODE_WIDTH, column, 0.0)
        )

    def process(k, block):
        arr[k] = block
        msg[k, :, cap_up:] = tail_msg[...]
        if cap_up > cap:
            msg[k, :, cap:cap_up] = jnp.zeros((8, cap_up - cap), F32)
        acts = forward(wt, m0, block)
        for h in range(2):
            raw = dot(tail_rows(wt, h), acts[h], NT)
            msg[k, 4 * h : 4 * h + 4, 0:cap] = raw[0:4]

    process(0, disp[me])
    back[me] = msg[0]

    def step(k, carry):
        out_copy(k).wait_recv()
        process(k, recv[k])
        back_copy(k).start()
        return carry

    lax.fori_loop(1, groups, step, 0)

    def finish(k, carry):
        out_copy(k).wait_send()
        back_copy(k).wait_send()
        back_copy(k).wait_recv()
        return carry

    lax.fori_loop(1, groups, finish, 0)
    raw_out[...] = back[...]


def home_kernel(
    groups, cap_up, slot_ref, raw_ref, cell_ref, spacing_ref, length_ref, target_ref, image_ref,
    code_ref, first_ref, second_ref, loss_out, msg_out, code_out, first_out, second_out,
    rows, table, eight, mix, queries, shift,
):
    tiles = cap_up // LANES
    filler = jnp.zeros((LANES - 8, LANES), F32)

    def widen(g, carry):
        for t in range(tiles):
            piece = raw_ref[g, :, t * LANES : (t + 1) * LANES]
            turned = jnp.concatenate([piece, filler], axis=0).T
            for h in range(2):
                start = pl.multiple_of((2 * g + h) * cap_up + t * LANES, LANES)
                table[pl.ds(start, LANES), :] = turned
        block = pl.ds(pl.multiple_of(8 * g, 8), 8)
        queries[block, :] = raw_ref[g, :, cap_up : cap_up + CODE_WIDTH]
        shift[block, :] = jnp.broadcast_to(
            raw_ref[g, :, cap_up + CODE_WIDTH : cap_up + CODE_WIDTH + 1], (8, LANES)
        )
        return carry

    lax.fori_loop(0, groups, widen, 0)
    table[pl.ds(2 * groups * cap_up, 8), :] = jnp.zeros((8, LANES), F32)

    def take(s):
        rows[pl.ds(s, 1), :] = table[pl.ds(slot_ref[s], 1), :]

    move_rows(rows.shape[0], take)

    def narrow(i):
        eight[pl.ds(pl.multiple_of(8 * i, 8), 8), :] = rows[lane_block(i), :].T[0:8]

    unrolled(SAMPLES, narrow)
    table[...] = jnp.zeros_like(table)

    table_rows = code_ref.shape[0]
    pick = (
        lax.broadcasted_iota(jnp.int32, (table_rows, LANES), 0) == image_ref[...]
    ).astype(F32)
    code_bf = code_ref[...].astype(BF16).astype(F32)
    ray_code = exact(code_bf, pick, TN)
    mix[...] = exact(queries[...], ray_code) + shift[...]

    cell = cell_ref[...]
    odd = lax.rem(cell, 2) == 1
    row = lax.broadcasted_iota(jnp.int32, (SAMPLES, LANES), 0)
    live = row < length_ref[...]
    raws = tuple(
        jnp.where(
            odd, eight[pl.ds(4 + c, SAMPLES, 8), :], eight[pl.ds(c, SAMPLES, 8), :]
        )
        for c in range(4)
    )

    def add_code(g, raws):
        part = mix[pl.ds(pl.multiple_of(8 * g, 8), 8), :]
        raws = list(raws)
        for h in range(2):
            hit = cell == 2 * g + h
            for c in range(4):
                j = 4 * h + c
                raws[c] = raws[c] + jnp.where(hit, part[j : j + 1, :], 0.0)
        return tuple(raws)

    raws = lax.fori_loop(0, groups, add_code, raws)
    raws = [jnp.where(live, raw, 0.0) for raw in raws]
    spacing = spacing_ref[...]
    density = jnp.maximum(raws[0], 0.0) + jnp.log1p(jnp.exp(-jnp.abs(raws[0])))
    colors = [jax.nn.sigmoid(raw) for raw in raws[1:]]
    tau = jnp.where(live, density * spacing, 0.0)
    square_row = lax.broadcasted_iota(jnp.int32, (SAMPLES, SAMPLES), 0)
    square_col = lax.broadcasted_iota(jnp.int32, (SAMPLES, SAMPLES), 1)
    before = exact((square_col < square_row).astype(F32), tau)
    through = jnp.exp(-before)
    fade = jnp.exp(-tau)
    weight = through * (1.0 - fade)
    gaps = [
        jnp.sum(weight * colors[c], axis=0, keepdims=True) - target_ref[c : c + 1, :]
        for c in range(3)
    ]
    loss_out[...] = 0.5 * (gaps[0] * gaps[0] + gaps[1] * gaps[1] + gaps[2] * gaps[2])
    pull = gaps[0] * colors[0] + gaps[1] * colors[1] + gaps[2] * colors[2]
    after = exact((square_col > square_row).astype(F32), pull * weight)
    tau_grad = pull * through * fade - after
    grads = [tau_grad * spacing * jax.nn.sigmoid(raws[0])]
    for c in range(3):
        grads.append(gaps[c] * weight * colors[c] * (1.0 - colors[c]))
    cots = [jnp.where(live, grad, 0.0).astype(BF16).astype(F32) for grad in grads]
    for c in range(4):
        eight[pl.ds(c, SAMPLES, 8), :] = jnp.where(odd, 0.0, cots[c])
        eight[pl.ds(4 + c, SAMPLES, 8), :] = jnp.where(odd, cots[c], 0.0)

    def gather_code(g, carry):
        pieces = []
        for h in range(2):
            hit = cell == 2 * g + h
            for c in range(4):
                pieces.append(jnp.sum(jnp.where(hit, cots[c], 0.0), axis=0, keepdims=True))
        mix[pl.ds(pl.multiple_of(8 * g, 8), 8), :] = jnp.concatenate(pieces, axis=0)
        return carry

    lax.fori_loop(0, groups, gather_code, 0)
    totals = mix[...]
    query_grad = exact(totals, ray_code, NT)
    table_grad = exact(exact(totals, pick, NT), queries[...], TN)
    new_code, new_first, new_second = adam_update(
        code_ref[...], table_grad, first_ref[...], second_ref[...]
    )
    code_out[...] = new_code
    first_out[...] = new_first
    second_out[...] = new_second
    queries[...] = query_grad

    def widen_back(i):
        piece = eight[pl.ds(pl.multiple_of(8 * i, 8), 8), :]
        rows[lane_block(i), :] = jnp.concatenate([piece, filler], axis=0).T

    unrolled(SAMPLES, widen_back)

    def put(s):
        table[pl.ds(slot_ref[s], 1), :] = rows[pl.ds(s, 1), :]

    move_rows(rows.shape[0], put)

    def pack(g, carry):
        for t in range(tiles):
            start = [pl.multiple_of((2 * g + h) * cap_up + t * LANES, LANES) for h in range(2)]
            both = table[pl.ds(start[0], LANES), :] + table[pl.ds(start[1], LANES), :]
            msg_out[g, :, t * LANES : (t + 1) * LANES] = both.T[0:8]
        part = queries[pl.ds(pl.multiple_of(8 * g, 8), 8), :]
        msg_out[g, :, cap_up:] = jnp.concatenate(
            [part, jnp.zeros((8, LANES - CODE_WIDTH), F32)], axis=1
        )
        return carry

    lax.fori_loop(0, groups, pack, 0)


def backward_kernel(
    groups, cap, cap_up, msg, wt, arr, grad_out, recv, act, pre, m0, turned, head, code_sum,
    cot_sum, bias, grad, half_in, sum_out, sum_in, full, s1, r1, s2, r2,
):
    me = lax.axis_index("expert")
    my_dp = lax.axis_index("dp")
    core = lax.rem(my_dp, 2)
    near = my_dp + 1 - 2 * core
    far = my_dp + 2 - 4 * lax.rem(my_dp // 2, 2)
    barrier = greet(groups, me)
    for peer in (near, far):
        pl.semaphore_signal(barrier, 1, device_id={"dp": peer}, device_id_type=MESH)
    pl.semaphore_wait(barrier, groups + 1)

    def out_copy(k):
        peer = lax.rem(me + k, groups)
        return pltpu.make_async_remote_copy(
            msg.at[peer], recv.at[k], s1.at[k], r1.at[k],
            device_id={"expert": peer}, device_id_type=MESH,
        )

    def start(k, carry):
        out_copy(k).start()
        return carry

    lax.fori_loop(1, groups, start, 0)
    pad_first(wt, m0)
    head[...] = jnp.zeros_like(head)
    bias[...] = jnp.zeros_like(bias)
    for h in range(2):
        head[h, 4 * h : 4 * h + 4, :] = tail_rows(wt, h).astype(F32)[0:4]
        for layer in range(1, LAYERS):
            matrix = layer_matrix(wt, m0, h, layer)
            turned[layer - 1, h] = matrix.astype(F32).T.astype(BF16)

    pieces = 4
    size = arr.shape[0] // pieces

    def piece(index):
        return pl.ds(pl.multiple_of(index * size, 16), size)

    def again(index, carry):
        block = piece(index)

        def keep(layer, h, value):
            act[layer, h, block, :] = value

        forward(wt, m0, arr[block, :], keep)
        return carry

    lax.fori_loop(0, pieces, again, 0)
    recv[0] = msg[me]

    def arrive(k, carry):
        out_copy(k).wait()
        return carry

    lax.fori_loop(1, groups, arrive, 0)

    starts = [0] + [ENC_WIDTH + layer * NET_WIDTH for layer in range(LAYERS)] + [HEAD_ROW + 16]
    chunks = [pl.ds(starts[j], starts[j + 1] - starts[j]) for j in range(LAYERS + 1)]

    def near_copy(j):
        return pltpu.make_async_remote_copy(
            grad.at[1 - core, chunks[j]], half_in.at[chunks[j]],
            s2.at[0, j], r2.at[0, j], device_id={"dp": near}, device_id_type=MESH,
        )

    def far_copy(j):
        return pltpu.make_async_remote_copy(
            sum_out.at[chunks[j]], sum_in.at[chunks[j]],
            s2.at[1, j], r2.at[1, j], device_id={"dp": far}, device_id_type=MESH,
        )

    def full_copy(j, which):
        return pltpu.make_async_remote_copy(
            full.at[which, chunks[j]], full.at[which, chunks[j]],
            s2.at[2, j], r2.at[2, j], device_id={"dp": near}, device_id_type=MESH,
        )

    def second_stage(j):
        near_copy(j).wait_recv()
        rows = chunks[j]
        sum_out[rows, :] = (grad[core, rows, :] + half_in[rows, :]).astype(BF16)
        far_copy(j).start()

    def third_stage(j):
        far_copy(j).wait_recv()
        rows = chunks[j]
        full[core, rows, :] = sum_out[rows, :].astype(F32) + sum_in[rows, :].astype(F32)
        full_copy(j, core).start()

    top = LAYERS - 1
    heads_bf = [head[h].astype(BF16) for h in range(2)]

    def mask_store(layer, h, block, up):
        value = jnp.where(act[layer, h, block, :].astype(F32) > 0, up, 0.0).astype(BF16)
        pre[layer, h, block, :] = value
        bias[layer, h] += jnp.sum(
            value.astype(F32).reshape(-1, 8, NET_WIDTH), axis=0
        )

    code_sum[...] = jnp.zeros_like(code_sum)
    cot_sum[...] = jnp.zeros_like(cot_sum)

    def first_back(k, carry):
        block = pl.ds(pl.multiple_of(k * cap, 16), cap)
        cot = recv[k, :, 0:cap].astype(BF16)
        sums = []
        for h in range(2):
            mask_store(top, h, block, dot(cot, heads_bf[h], TN))
            sums.append(carry[h] + dot(cot, act[top, h, block, :]))
        code_sum[...] += recv[k, :, cap_up:]
        cot_sum[...] += jnp.broadcast_to(
            jnp.sum(recv[k, :, 0:cap], axis=1, keepdims=True), (8, LANES)
        )
        return tuple(sums)

    hidden = lax.fori_loop(
        0, groups, first_back, (jnp.zeros((8, NET_WIDTH), F32), jnp.zeros((8, NET_WIDTH), F32))
    )

    for layer in reversed(range(LAYERS)):
        if layer < top:

            def back(index, carry):
                block = piece(index)
                for h in range(2):
                    mask_store(
                        layer, h, block, dot(pre[layer + 1, h, block, :], turned[layer, h])
                    )
                return carry

            lax.fori_loop(0, pieces, back, 0)
        for h in range(2):
            if layer == 0:
                value = dot(arr[...], pre[0, h], TN)
                grad[h, 0:ENC_WIDTH, :] = value[ENC_WIDTH * h : ENC_WIDTH * (h + 1)]
            else:
                grad[h, chunks[layer], :] = dot(act[layer - 1, h], pre[layer, h], TN)
        near_copy(layer).start()
        if layer < top:
            second_stage(layer + 1)
        if layer < top - 1:
            third_stage(layer + 2)

    codes = jnp.concatenate([code_sum[...], jnp.zeros((8, NET_WIDTH - LANES), F32)], axis=1)
    spot = (
        lax.broadcasted_iota(jnp.int32, (8, LANES), 0)
        == lax.broadcasted_iota(jnp.int32, (8, LANES), 1)
    )
    cot_row = jnp.sum(jnp.where(spot, cot_sum[...], 0.0), axis=0, keepdims=True)
    lane = lax.broadcasted_iota(jnp.int32, (1, LANES), 1)
    for h in range(2):
        line = cot_row if h == 0 else pltpu.roll(cot_row, LANES - 4, 1)
        line = jnp.where(lane < 4, line, 0.0)
        line = jnp.concatenate([line, jnp.zeros((1, NET_WIDTH - LANES), F32)], axis=1)
        grad[h, HEAD_ROW : HEAD_ROW + 16, :] = jnp.concatenate(
            [hidden[h][4 * h : 4 * h + 4], codes[4 * h : 4 * h + 4], line]
            + [jnp.sum(bias[layer, h], axis=0, keepdims=True) for layer in range(LAYERS)]
            + [jnp.zeros((7 - LAYERS, NET_WIDTH), F32)],
            axis=0,
        )
    near_copy(LAYERS).start()
    second_stage(0)
    third_stage(1)
    second_stage(LAYERS)
    third_stage(0)
    third_stage(LAYERS)
    for j in (3, 2, 1, 0, LAYERS):
        near_copy(j).wait_send()
        far_copy(j).wait_send()
        full_copy(j, core).wait_send()
        full_copy(j, 1 - core).wait_recv()
        grad_out[:, chunks[j], :] = full[:, chunks[j], :]


def shards(
    features, spacing, targets, ray_length, cell_id, slot_rank, image_id,
    params, first_moment, second_moment, code_table, table_first, table_second,
):
    ray_rows = features.shape[0]
    sample_count = ray_rows * SAMPLES
    groups = lax.axis_size("expert")
    experts_all = params.shape[0] * groups
    cap = 2 * (sample_count * 3 // 4 // experts_all)
    cap_up = -(-cap // LANES) * LANES
    width = cap_up + LANES
    slots_up = experts_all * cap_up
    table_rows = code_table.shape[0]
    block_index = lax.axis_index("expert") * lax.axis_size("dp") + lax.axis_index("dp")
    local_image = (image_id - block_index * table_rows)[None, :]
    cell = cell_id.T
    rank = slot_rank.T
    slot = jnp.where(rank >= 0, cell * cap_up + rank, slots_up).reshape(sample_count)
    shape = jax.ShapeDtypeStruct
    big = 46 * 2**20
    table_scratch = pltpu.VMEM((slots_up + 8, LANES), F32)
    rows_scratch = pltpu.VMEM((sample_count, LANES), F32)
    msg_shape = (groups, 8, width)
    local = (sample_count + slots_up) * LANES * 4 + 8 * 2**20
    disp = pl.pallas_call(
        functools.partial(place_kernel, groups, cap, cap_up),
        out_shape=shape((groups, cap, LANES), BF16),
        in_specs=[SMEM, VMEM],
        out_specs=VMEM,
        scratch_shapes=[rows_scratch, table_scratch],
        compiler_params=pltpu.CompilerParams(vmem_limit_bytes=local),
        cost_estimate=pl.CostEstimate(flops=0, bytes_accessed=6000 * sample_count, transcendentals=0),
        name="place",
    )(slot, features.transpose(1, 2, 0))
    sems = pltpu.SemaphoreType.DMA((groups,))
    arr, raw_back, weights_bf = pl.pallas_call(
        functools.partial(forward_kernel, groups, cap, cap_up),
        out_shape=(
            shape((groups, cap, LANES), BF16), shape(msg_shape, F32), shape(params.shape, BF16),
        ),
        in_specs=[VMEM, pl.BlockSpec(memory_space=pltpu.HBM)],
        out_specs=(VMEM,) * 3,
        scratch_shapes=[
            pltpu.VMEM((groups, cap, LANES), BF16),
            pltpu.VMEM(msg_shape, F32),
            pltpu.VMEM(msg_shape, F32),
            pltpu.VMEM((2, LANES, NET_WIDTH), BF16),
            pltpu.VMEM((8, LANES), F32),
            pltpu.VMEM(params.shape, F32),
            pltpu.SemaphoreType.DMA,
            sems, sems, sems, sems,
        ],
        compiler_params=pltpu.CompilerParams(
            collective_id=0, has_side_effects=True, vmem_limit_bytes=32 * 2**20
        ),
        cost_estimate=pl.CostEstimate(flops=0, bytes_accessed=16000 * sample_count, transcendentals=0),
        name="dispatch",
    )(disp, params)
    table_shape = shape(code_table.shape, F32)
    loss, cot_msg, new_table, new_table_first, new_table_second = pl.pallas_call(
        functools.partial(home_kernel, groups, cap_up),
        out_shape=(
            shape((1, ray_rows), F32), shape(msg_shape, F32), table_shape, table_shape, table_shape,
        ),
        in_specs=[SMEM] + [VMEM] * 9,
        out_specs=(VMEM,) * 5,
        scratch_shapes=[
            rows_scratch,
            table_scratch,
            pltpu.VMEM((8 * SAMPLES, LANES), F32),
            pltpu.VMEM((8 * groups, LANES), F32),
            pltpu.VMEM((8 * groups, CODE_WIDTH), F32),
            pltpu.VMEM((8 * groups, LANES), F32),
        ],
        compiler_params=pltpu.CompilerParams(vmem_limit_bytes=local),
        cost_estimate=pl.CostEstimate(flops=0, bytes_accessed=12000 * sample_count, transcendentals=0),
        name="home",
    )(
        slot, raw_back, cell, spacing.T, ray_length[None, :], targets, local_image,
        code_table, table_first, table_second,
    )
    all_rows = groups * cap
    grad_rows = params.shape[1]
    param_grad = pl.pallas_call(
        functools.partial(backward_kernel, groups, cap, cap_up),
        out_shape=shape(params.shape, F32),
        in_specs=[VMEM] * 3,
        out_specs=VMEM,
        scratch_shapes=[
            pltpu.VMEM(msg_shape, F32),
            pltpu.VMEM((LAYERS, 2, all_rows, NET_WIDTH), BF16),
            pltpu.VMEM((LAYERS, 2, all_rows, NET_WIDTH), BF16),
            pltpu.VMEM((2, LANES, NET_WIDTH), BF16),
            pltpu.VMEM((LAYERS - 1, 2, NET_WIDTH, NET_WIDTH), BF16),
            pltpu.VMEM((2, 8, NET_WIDTH), F32),
            pltpu.VMEM((8, LANES), F32),
            pltpu.VMEM((8, LANES), F32),
            pltpu.VMEM((LAYERS, 2, 8, NET_WIDTH), F32),
            pltpu.VMEM((2, grad_rows, NET_WIDTH), F32),
            pltpu.VMEM((grad_rows, NET_WIDTH), F32),
            pltpu.VMEM((grad_rows, NET_WIDTH), BF16),
            pltpu.VMEM((grad_rows, NET_WIDTH), BF16),
            pltpu.VMEM((2, grad_rows, NET_WIDTH), F32),
            sems, sems,
            pltpu.SemaphoreType.DMA((3, LAYERS + 1)),
            pltpu.SemaphoreType.DMA((3, LAYERS + 1)),
        ],
        compiler_params=pltpu.CompilerParams(
            collective_id=1, has_side_effects=True, vmem_limit_bytes=big
        ),
        cost_estimate=pl.CostEstimate(flops=0, bytes_accessed=20000 * sample_count, transcendentals=0),
        name="backward",
    )(cot_msg, weights_bf, arr.reshape(all_rows, LANES))
    new_params, new_first, new_second = adam_update(params, param_grad, first_moment, second_moment)
    return (
        loss.reshape(ray_rows), new_params, new_first, new_second,
        new_table, new_table_first, new_table_second,
    )


def solution(mesh):
    both = ("expert", "dp")
    return jax.shard_map(
        shards,
        mesh=mesh,
        in_specs=(
            P(both, None, None), P(both, None), P(None, both), P(both), P(both, None),
            P(both, None), P(both),
            P("expert", None, None), P("expert", None, None), P("expert", None, None),
            P(both, None), P(both, None), P(both, None),
        ),
        out_specs=(
            P(both),
            P("expert", None, None), P("expert", None, None), P("expert", None, None),
            P(both, None), P(both, None), P(both, None),
        ),
        check_vma=False,
    )
```
